256 devices in a mesh: rep: 2 (over core), exp: 128 (over x, y, z).
Axes of the slice: x: 4, y: 4, z: 8, core: 2. Of those that a mesh axis runs over, the one named last changes fastest.
Arguments:
- attn_out: bfloat16 [16384, 4096], P(('rep', 'exp')), may hold values from -6 to 6
- out_weight: bfloat16 [4096, 2048], P('exp'), may hold values from -0.09375 to 0.09375
- router_weight: bfloat16 [2048, 128], replicated, may hold values from -0.125 to 0.125
- gate_weight: bfloat16 [128, 2048, 768], P('exp'), may hold values from -0.125 to 0.125
- up_weight: bfloat16 [128, 2048, 768], P('exp'), may hold values from -0.125 to 0.125
- down_weight: bfloat16 [128, 768, 2048], P('exp'), may hold values from -0.21875 to 0.21875
- cotangent: bfloat16 [16384, 2048], P(('rep', 'exp')), may hold values from -6 to 6
- log_ratios: float32 [16384], P(('rep', 'exp')), may hold values from -0.03 to 0.05
- expert_ids: int32 [16384, 8], P(('rep', 'exp')), may hold values from 0 to 127, as said below
- slot_ids: int32 [16384, 8], P(('rep', 'exp')), may hold values from 0 to 5, as said below
- episode_ids: int32 [16384], P(('rep', 'exp')), may hold values from 0 to 255, never falling along the last dimension, each value on 1 to 256 neighbouring positions
Outputs:
- token_grads: bfloat16 [16384, 4096], P(('rep', 'exp'))
- router_grad: float32 [2048, 128], P('exp')
The draws below stay inside these ranges and needn't reach their ends.
Inputs may be any that keep to these rules, and one draw needn't show every extreme that they name: `expert_ids`: each row names 8 different experts. Among the rows of one device no expert is named more than 6 times, and on every device some expert is named exactly 6 times. `slot_ids`: among the rows of one device, the pairs of a row with one expert named in it get distinct slots; the slots of one expert on one device are 0 up to the number of its pairs there minus 1. `episode_ids`: episodes are runs of consecutive tokens, numbered in order; each has 1 to 256 tokens, one exactly 256.
All inputs are finite; a program needn't handle non-finite values.
Results may differ from the reference program's by a relative error of at most 0.012.
Values may be sent and summed in bfloat16 or wider, within the bound.
No kernel may reach another device: no remote copies, remote signals or barrier semaphores. Data moves between devices by JAX's collectives and lax.ppermute only.
A program may use at most 128 MiB of HBM per device.

```python
import math
import jax
import jax.numpy as jnp
import numpy as np
from jax import lax

D = 2048
DA = 4096
FF = 768
TOPK = 8
TOK_DEV = 64
EP_MOST = 256
EXPERTS = 128
TOKENS = 16384
CAP = 6
EPISODES = 256


def route_tables(key):
    blocks = TOKENS // TOK_DEV
    pairs = TOK_DEV * TOPK
    popularity = jax.random.randint(jax.random.fold_in(key, 11), (EXPERTS,), 0, 40)

    def one_block(block_key):
        noise_key = jax.random.fold_in(block_key, 1)
        forced_key = jax.random.fold_in(block_key, 2)
        order_key = jax.random.fold_in(block_key, 3)
        block_noise = jax.random.randint(noise_key, (EXPERTS,), 0, 10)
        forced = jax.random.randint(forced_key, (), 0, EXPERTS)
        expert_range = jnp.arange(EXPERTS, dtype=jnp.int32)
        popular = popularity + block_noise + jnp.where(expert_range == forced, 100000, 0)
        slot_level = jnp.arange(CAP, dtype=jnp.int32)
        pair_score = (popular[:, None] - 10 * slot_level[None, :]) * EXPERTS + expert_range[:, None]
        cutoff = lax.top_k(pair_score.reshape(-1), pairs)[0][pairs - 1]
        picked = (pair_score >= cutoff).astype(jnp.int32)
        counts = jnp.sum(picked, axis=1)
        run_ends = jnp.cumsum(counts)
        run_starts = run_ends - counts
        positions = jnp.arange(pairs, dtype=jnp.int32)
        run_owner = jnp.sum((run_ends[None, :] <= positions[:, None]).astype(jnp.int32), axis=1)
        owner_start = jnp.sum(jnp.where(expert_range[None, :] == run_owner[:, None], run_starts[None, :], 0), axis=1)
        slot_number = positions - owner_start
        ids_table = run_owner.reshape(TOPK, TOK_DEV).T
        slots_table = slot_number.reshape(TOPK, TOK_DEV).T
        token_order = jax.random.permutation(order_key, TOK_DEV)
        return (ids_table[token_order], slots_table[token_order])
    block_keys = jax.random.split(jax.random.fold_in(key, 7), blocks)
    ids_all, slots_all = jax.vmap(one_block)(block_keys)
    return (ids_all.reshape(TOKENS, TOPK).astype(jnp.int32), slots_all.reshape(TOKENS, TOPK).astype(jnp.int32))


def draw_expert_ids(key, part):
    return route_tables(key)[0]


def draw_slot_ids(key, part):
    return route_tables(key)[1]


def levels(own_key, extent, pieces, least, high):
    gain = 1.0
    for axis_at, parts in pieces:
        heights = jax.random.uniform(jax.random.fold_in(jax.random.fold_in(own_key, 6), axis_at), (parts,), jnp.float32, least / len(pieces), high / len(pieces))
        gain = gain * jnp.repeat(jnp.exp(heights), extent[axis_at] // parts).reshape((-1,) + (1,) * (len(extent) - 1 - axis_at))
    return gain


def split_up(amount, total, limit, slope):
    weights = [(1 << 20) // math.isqrt(standing ** slope) + 1 for standing in range(2, amount + 1)]
    spare, given = total - limit - (amount - 1), [1] * (amount - 1)
    while spare > 0:
        candidates = [i for i in range(amount - 1) if given[i] < limit]
        mass, left = sum([weights[i] for i in candidates]), spare
        for i in candidates:
            addition = min(limit - given[i], max(1, left * weights[i] // mass), spare)
            given[i] = given[i] + addition
            spare = spare - addition
    return np.array([limit] + given)


def ragged_sizes(rng, count, total, bound, skew):
    if count == 2:
        one = jax.random.randint(rng, (), max(1, total - bound), min(bound, total - 1) + 1)
        return jnp.stack([one, total - one])
    lengths = jnp.asarray(split_up(count, total, bound, skew), jnp.int32)
    pairs = (count - 1) // 2
    donor, receiver = lengths[1:1 + 2 * pairs:2], lengths[2:2 + 2 * pairs:2]
    room = jnp.minimum(donor - 1, bound - receiver)
    passed = jax.random.randint(jax.random.fold_in(rng, 1), (pairs,), 0, 1 << 20) % (room + 1)
    lengths = lengths.at[1:1 + 2 * pairs:2].set(donor - passed).at[2:2 + 2 * pairs:2].set(receiver + passed)
    return lengths[jax.random.permutation(jax.random.fold_in(rng, 2), count)]


def normal_values(own_key, dims, spread, bound, pieces=(), kind=jnp.bfloat16):
    gain = levels(own_key, dims, pieces, -0.22, 0.18) if pieces else 1.0
    array = jax.random.normal(own_key, dims, jnp.float32) * spread * gain
    return jnp.minimum(jnp.maximum(array, -bound), bound).astype(kind)


def setup_inputs(seed: int = 0) -> dict:
    arg_keys = jax.random.split(jax.random.key(seed), 12)
    attn_out = normal_values(arg_keys[0], (TOKENS, DA), 1.0, 6.0, ((0, 256),))
    out_weight = normal_values(arg_keys[1], (DA, D), DA ** -0.5, 0.09375, ((0, 128),))
    router_weight = normal_values(arg_keys[2], (D, EXPERTS), D ** -0.5, 0.125)
    gate_weight = normal_values(arg_keys[3], (EXPERTS, D, FF), D ** -0.5, 0.125, ((0, 128),))
    up_weight = normal_values(arg_keys[4], (EXPERTS, D, FF), D ** -0.5, 0.125, ((0, 128),))
    down_weight = normal_values(arg_keys[5], (EXPERTS, FF, D), FF ** -0.5, 0.21875, ((0, 128),))
    cotangent = normal_values(arg_keys[6], (TOKENS, D), 1.0, 6.0, ((0, 256),))
    log_ratios = jnp.clip(-0.03 + 0.08 * jax.random.uniform(arg_keys[7], (TOKENS,), jnp.float32) ** levels(arg_keys[7], (TOKENS,), ((0, 256),), -0.2, 0.2), -0.03, 0.05)
    expert_ids = draw_expert_ids(jax.random.fold_in(arg_keys[11], 71), 0)
    slot_ids = draw_slot_ids(jax.random.fold_in(arg_keys[11], 71), 0)
    episode_ids = jnp.searchsorted(jnp.cumsum(ragged_sizes(arg_keys[10], EPISODES, TOKENS, EP_MOST, 2)), jnp.arange(TOKENS), side="right").astype(jnp.int32)
    return dict(attn_out=attn_out, out_weight=out_weight, router_weight=router_weight, gate_weight=gate_weight, up_weight=up_weight, down_weight=down_weight, cotangent=cotangent, log_ratios=log_ratios, expert_ids=expert_ids, slot_ids=slot_ids, episode_ids=episode_ids)


clip_top = 4.0


def reference(attn_out, out_weight, router_weight, gate_weight, up_weight, down_weight, cotangent, log_ratios, expert_ids, slot_ids, episode_ids):
    hidden = jnp.dot(attn_out, out_weight, preferred_element_type=jnp.float32).astype(jnp.bfloat16)
    logits = jnp.dot(hidden, router_weight, preferred_element_type=jnp.float32)
    chosen = jnp.take_along_axis(logits, expert_ids, axis=1)
    raised = jnp.exp(chosen)
    gate_probs = raised / jnp.sum(raised, axis=1, keepdims=True)
    log_sums = jax.ops.segment_sum(log_ratios, episode_ids, num_segments=EPISODES)
    counts = jax.ops.segment_sum(jnp.ones_like(log_ratios), episode_ids, num_segments=EPISODES)
    episode_weight = jnp.minimum(jnp.exp(log_sums), clip_top)
    mean_weight = jnp.sum(counts * episode_weight) / TOKENS
    token_scale = episode_weight[episode_ids] / mean_weight
    blocks = TOKENS // TOK_DEV
    source = (jnp.arange(TOKENS, dtype=jnp.int32) // TOK_DEV)[:, None]
    target = (expert_ids * blocks + source) * CAP + slot_ids
    labels = jnp.arange(TOKENS * TOPK, dtype=jnp.int32).reshape(TOKENS, TOPK) + 1
    slot_table = jnp.zeros((EXPERTS * blocks * CAP,), jnp.int32).at[target.reshape(-1)].set(labels.reshape(-1))
    slot_table = slot_table.reshape(EXPERTS, blocks * CAP)
    flat_gates = gate_probs.reshape(-1)

    def per_expert(carried, inputs):
        summed, scores = carried
        w_gate, w_up, w_down, labels_row = inputs
        filled = labels_row > 0
        pair_index = jnp.maximum(labels_row - 1, 0)
        token_index = pair_index // TOPK
        rows_in = jnp.where(filled[:, None], hidden[token_index], jnp.zeros((), jnp.bfloat16))
        cot_in = jnp.where(filled[:, None], cotangent[token_index], jnp.zeros((), jnp.bfloat16))
        gate_pre = jnp.dot(rows_in, w_gate, preferred_element_type=jnp.float32)
        up_pre = jnp.dot(rows_in, w_up, preferred_element_type=jnp.float32)
        upstream = jnp.dot(cot_in, w_down.T, preferred_element_type=jnp.float32)
        sigmoid_gate = jax.nn.sigmoid(gate_pre)
        slot_score = jnp.sum(upstream * (gate_pre * sigmoid_gate * up_pre), axis=1)
        grad_gate = (upstream * up_pre * sigmoid_gate * (1.0 + gate_pre * (1.0 - sigmoid_gate))).astype(jnp.bfloat16)
        grad_up = (upstream * gate_pre * sigmoid_gate).astype(jnp.bfloat16)
        back_rows = (jnp.dot(grad_gate, w_gate.T, preferred_element_type=jnp.float32) + jnp.dot(grad_up, w_up.T, preferred_element_type=jnp.float32)).astype(jnp.bfloat16)
        gate_rows = jnp.where(filled, flat_gates[pair_index], 0.0)
        summed = summed.at[token_index].add(gate_rows[:, None] * back_rows.astype(jnp.float32))
        scores = scores.at[pair_index].add(jnp.where(filled, slot_score, 0.0))
        return (summed, scores), None

    start_carry = (jnp.zeros((TOKENS, D), jnp.float32), jnp.zeros((TOKENS * TOPK,), jnp.float32))
    (summed, scores), unused = lax.scan(per_expert, start_carry, (gate_weight, up_weight, down_weight, slot_table))
    scores = scores.reshape(TOKENS, TOPK)
    logit_grad = gate_probs * (scores - jnp.sum(gate_probs * scores, axis=1, keepdims=True))
    expert_hits = (expert_ids[:, :, None] == jnp.arange(EXPERTS, dtype=jnp.int32)).astype(jnp.float32)
    full_grad = jnp.sum(expert_hits * logit_grad[:, :, None], axis=1)
    weighted = (token_scale[:, None] * full_grad).astype(jnp.bfloat16)
    router_grad = jnp.dot(hidden.T, weighted, preferred_element_type=jnp.float32)
    grad_hidden = (token_scale[:, None] * summed + jnp.dot(weighted, router_weight.T, preferred_element_type=jnp.float32)).astype(jnp.bfloat16)
    token_grads = jnp.dot(grad_hidden, out_weight.T, preferred_element_type=jnp.float32).astype(jnp.bfloat16)
    return (token_grads, router_grad)
```

```python
import jax
import jax.numpy as jnp
from jax import lax
from jax.sharding import Mesh, PartitionSpec as P

clip_top = 4.0
bf16 = jnp.bfloat16
f32 = jnp.float32


def shift(value, axis, step):
    count = lax.axis_size(axis)
    return lax.ppermute(value, axis, [(i, (i + step) % count) for i in range(count)])


def swap(value, axis, bit):
    count = lax.axis_size(axis)
    return lax.ppermute(value, axis, [(i, i ^ bit) for i in range(count)])


def butterfly_sum(value, axis):
    bit = 1
    while bit < lax.axis_size(axis):
        value = value + swap(value, axis, bit)
        bit *= 2
    return value


def butterfly_gather(value, axis, dim):
    me = lax.axis_index(axis)
    bit = 1
    while bit < lax.axis_size(axis):
        other = swap(value, axis, bit)
        low = (me & bit) == 0
        value = jnp.concatenate([jnp.where(low, value, other), jnp.where(low, other, value)], dim)
        bit *= 2
    return value


def ring_gather(value, axis, dim):
    count = lax.axis_size(axis)
    me = lax.axis_index(axis)
    shape = value.shape[:dim] + (count,) + value.shape[dim:]
    out = jnp.zeros(shape, value.dtype)

    def put(out, part, owner, start=0):
        at = [0] * len(shape)
        at[dim] = owner % count
        if start:
            at[1 if dim == 0 else 0] = start
        return lax.dynamic_update_slice(out, jnp.expand_dims(part, dim), at)

    out = put(out, value, me)
    up = down = value
    for step in range(1, count // 2):
        up = shift(up, axis, 1)
        down = shift(down, axis, -1)
        out = put(out, up, me - step + count)
        out = put(out, down, me + step)
    half = value.shape[0] // 2
    up = shift(up[:half], axis, 1)
    down = shift(down[half:], axis, -1)
    out = put(out, up, me + count // 2)
    return put(out, down, me + count // 2, half)


def ring_scatter(parts, axis):
    count = lax.axis_size(axis)
    me = lax.axis_index(axis)
    half = parts.shape[2] // 2

    def part(step):
        return lax.dynamic_index_in_dim(parts, (me + step + count) % count, 0, keepdims=False)

    far = part(count // 2).astype(bf16)
    up = shift(far[:, :half], axis, 1)
    down = shift(far[:, half:], axis, -1)
    for step in range(count // 2 - 1, 0, -1):
        own_up, own_down = part(step), part(-step)
        if up.shape[1] == half:
            own_up = jnp.concatenate([own_up[:, :half] + up.astype(f32), own_up[:, half:]], 1)
            own_down = jnp.concatenate(
                [own_down[:, :half], own_down[:, half:] + down.astype(f32)], 1
            )
        else:
            own_up = own_up + up.astype(f32)
            own_down = own_down + down.astype(f32)
        up = shift(own_up.astype(bf16), axis, 1)
        down = shift(own_down.astype(bf16), axis, -1)
    return part(0) + up.astype(f32) + down.astype(f32)


def plane_exchange(value):
    return lax.all_to_all(value, ("x", "y"), split_axis=0, concat_axis=0, tiled=True)


def dot(a, b, dims):
    return lax.dot_general(a, b, (dims, ((), ())), preferred_element_type=f32)


def shards(
    attn_out,
    out_weight,
    router_weight,
    gate_weight,
    up_weight,
    down_weight,
    cotangent,
    log_ratios,
    expert_ids,
    slot_ids,
    episode_ids,
):
    tok_count, attn_width = attn_out.shape
    top_count = expert_ids.shape[1]
    width = cotangent.shape[1]
    line = lax.axis_size("z")
    plane = lax.axis_size("x") * lax.axis_size("y")
    expert_count = plane * line
    device_count = lax.axis_size("rep") * expert_count
    capacity = 3 * tok_count * top_count // (2 * expert_count)
    episode_count = tok_count * device_count // 64
    rep = lax.axis_index("rep")
    level = lax.axis_index("z")
    slots = line * capacity
    line_toks = line * tok_count
    half = width // 2
    quarter = half // 2
    first = rep == 0

    codes = jnp.concatenate([expert_ids.T * capacity + slot_ids.T, episode_ids[None, :]], 0)
    codes = butterfly_gather(codes, "z", 1)
    line_episodes = codes[top_count:]
    codes = codes[:top_count]
    experts = codes // capacity
    source = jnp.arange(line_toks, dtype=jnp.int32)[None, :] // tok_count
    targets = (experts // line) * slots + source * capacity + codes % capacity
    targets = jnp.where(experts % line == level, targets, -1)
    slot_range = jnp.arange(plane * slots, dtype=jnp.int32)[:, None]
    picks = (targets[0:1] == slot_range).astype(f32)
    for k in range(1, top_count):
        picks = picks + (targets[k : k + 1] == slot_range).astype(f32)
    select = picks.astype(bf16)

    hits = jnp.arange(episode_count, dtype=jnp.int32)[:, None] == episode_ids[None, :]
    sums = jnp.stack(
        [
            jnp.sum(jnp.where(hits, log_ratios[None, :], 0.0), axis=1),
            jnp.sum(hits.astype(f32), axis=1),
        ]
    )
    for axis in ("z", "y", "x", "rep"):
        sums = butterfly_sum(sums, axis)
    episode_weight = jnp.minimum(jnp.exp(sums[0]), clip_top)
    mean_weight = jnp.sum(sums[1] * episode_weight) / (tok_count * device_count)
    line_hits = jnp.arange(episode_count, dtype=jnp.int32)[:, None] == line_episodes
    line_scale = (
        jnp.sum(jnp.where(line_hits, episode_weight[:, None], 0.0), axis=0) / mean_weight
    )

    attn_other = swap(attn_out, "rep", 1)
    own_cols = lax.dynamic_slice_in_dim(out_weight, rep * half, half, 1)
    cols = ring_gather(own_cols, "z", 0)
    cols_a = ring_gather(ring_gather(cols[:, :, :quarter], "y", 0), "x", 0)
    cols_b = ring_gather(ring_gather(cols[:, :, quarter:], "x", 0), "y", 1)
    cols_a = cols_a.reshape(attn_width, quarter)
    cols_b = cols_b.reshape(attn_width, quarter)
    attn_both = jnp.concatenate([attn_out, attn_other], 0)
    mm = ((1,), (0,))
    mt = ((1,), (1,))
    hidden_half = jnp.concatenate([dot(attn_both, cols_a, mm), dot(attn_both, cols_b, mm)], 1)
    hidden_half = hidden_half.astype(bf16)
    got = swap(hidden_half[tok_count:], "rep", 1)
    mine = hidden_half[:tok_count]
    hidden = jnp.concatenate([jnp.where(first, mine, got), jnp.where(first, got, mine)], 1)

    line_cot = ring_gather(cotangent, "z", 0).reshape(line_toks, width)
    send_cot = dot(select, line_cot, mm).astype(bf16).reshape(plane, slots, width)
    cot_in = plane_exchange(send_cot).reshape(plane * slots, width)
    line_hidden = ring_gather(hidden, "z", 0).reshape(line_toks, width)
    send_hidden = dot(select, line_hidden, mm).astype(bf16).reshape(plane, slots, width)
    rows_in = plane_exchange(send_hidden).reshape(plane * slots, width)

    logits = dot(router_weight, line_hidden, ((0,), (1,)))
    expert_range = jnp.arange(expert_count, dtype=jnp.int32)[:, None]
    named = experts[0:1] == expert_range
    for k in range(1, top_count):
        named = named | (experts[k : k + 1] == expert_range)
    raised = jnp.where(named, jnp.exp(jnp.where(named, logits, 0.0)), 0.0)
    probs = raised / jnp.sum(raised, axis=0, keepdims=True)
    here = jnp.arange(line, dtype=jnp.int32)[None, :, None] == level
    plane_probs = jnp.sum(jnp.where(here, probs.reshape(plane, line, line_toks), 0.0), axis=1)

    gate_pre = dot(rows_in, gate_weight[0], mm)
    up_pre = dot(rows_in, up_weight[0], mm)
    upstream = dot(cot_in, down_weight[0], mt)
    sigmoid_gate = jax.nn.sigmoid(gate_pre)
    slot_score = jnp.sum(upstream * (gate_pre * sigmoid_gate * up_pre), axis=1)
    grad_gate = (upstream * up_pre * sigmoid_gate * (1.0 + gate_pre * (1.0 - sigmoid_gate))).astype(
        bf16
    )
    grad_up = (upstream * gate_pre * sigmoid_gate).astype(bf16)
    back_rows = (dot(grad_gate, gate_weight[0], mt) + dot(grad_up, up_weight[0], mt)).astype(bf16)
    score_home = plane_exchange(slot_score.reshape(plane, slots))
    back_home = plane_exchange(back_rows.reshape(plane, slots, width))

    picks = picks.reshape(plane, slots, line_toks)
    plane_scores = jnp.sum(picks * score_home[:, :, None], axis=1)
    score_sum = butterfly_sum(jnp.sum(plane_probs * plane_scores, axis=0), "z")
    logit_grad = plane_probs * (plane_scores - score_sum[None, :])
    weighted = (line_scale[None, :] * logit_grad).astype(bf16)

    router_part = dot(weighted, line_hidden, mm).reshape(plane, plane, width // plane)
    router_part = jnp.sum(plane_exchange(router_part.transpose(1, 0, 2)), axis=0)
    router_part = router_part + swap(router_part, "rep", 1)
    router_all = butterfly_gather(router_part[None], "z", 0)
    rows = width // expert_count
    router_own = lax.dynamic_slice_in_dim(router_all, level * rows, rows, 2)
    router_grad = router_own.transpose(2, 1, 0).reshape(rows, expert_count)

    mix = picks * (plane_probs * line_scale[None, :])[:, None, :]
    mix = mix.reshape(plane * slots, line_toks).astype(bf16)
    here_experts = jnp.arange(plane, dtype=jnp.int32)[:, None] * line + level
    plane_router = dot(
        (here_experts == jnp.arange(expert_count, dtype=jnp.int32)[None, :]).astype(bf16),
        router_weight,
        mt,
    ).astype(bf16)
    tm = ((0,), (0,))
    parts = dot(mix, back_home.reshape(plane * slots, width), tm) + dot(weighted, plane_router, tm)
    grad_hidden = ring_scatter(parts.reshape(line, tok_count, width), "z").astype(bf16)

    low, high = grad_hidden[:, :half], grad_hidden[:, half:]
    keep = jnp.where(first, low, high)
    other = swap(jnp.where(first, high, low), "rep", 1)

    def project(rows):
        return dot(rows[:, :quarter], cols_a, mt) + dot(rows[:, quarter:], cols_b, mt)

    back_other = swap(project(other).astype(bf16), "rep", 1)
    token_grads = (project(keep) + back_other.astype(f32)).astype(bf16)
    return (token_grads, router_grad)


def solution(mesh):
    grid = Mesh(mesh.devices.reshape(2, 4, 4, 8), ("rep", "x", "y", "z"))
    exp = ("x", "y", "z")
    every = ("rep",) + exp
    placed = (
        P(every, None),
        P(exp, None),
        P(),
        P(exp, None, None),
        P(exp, None, None),
        P(exp, None, None),
        P(every, None),
        P(every),
        P(every, None),
        P(every, None),
        P(every),
    )
    return jax.shard_map(
        shards,
        mesh=grid,
        in_specs=placed,
        out_specs=(P(every, None), P(exp, None)),
        check_vma=False,
    )
```
